512 devices in a mesh: ctx: 64 (over y, z_lo, x), mp: 8 (over z_hi, core).
Axes of the slice: x: 4, y: 8, z: 8 (z_hi: 4, z_lo: 2; z = z_hi * 2 + z_lo), core: 2. Of those that a mesh axis runs over, the one named last changes fastest.
Arguments:
- queries: bfloat16 [16384, 8192], P('ctx', 'mp'), may hold values from -6 to 6
- key_feats: bfloat16 [16384, 8192], P('ctx', 'mp'), may hold values from -6 to 6
- value_feats: bfloat16 [16384, 8192], P('ctx', 'mp'), may hold values from -6 to 6
- filters: bfloat16 [512, 128], P('mp'), may hold values from -0.5 to 0.5
- grad_out: bfloat16 [16384, 8192], P('ctx', 'mp'), may hold values from -40 to 40
Outputs:
- mixer_out: bfloat16 [16384, 8192], P('ctx', 'mp')
- grad_queries: bfloat16 [16384, 8192], P('ctx', 'mp')
- grad_keys: bfloat16 [16384, 8192], P('ctx', 'mp')
- grad_values: bfloat16 [16384, 8192], P('ctx', 'mp')
- grad_filters: float32 [512, 128], P('mp')
The draws below stay inside these ranges and needn't reach their ends.
All inputs are finite; a program needn't handle non-finite values.
Results may differ from the reference program's by a relative error of at most 0.0058.
Values may be sent and summed in bfloat16 or wider, within the bound.
No kernel may reach another device: no remote copies, remote signals or barrier semaphores. Data moves between devices by JAX's collectives and lax.ppermute only.
A program may use at most 64 MiB of HBM per device.

```python
import jax
import jax.numpy as jnp
from jax import lax

D = 8192
G = 16
K = 128
LENGTH = 16384
GROUPS = 512


def draw_grad_out(key, part):
    first_key = jax.random.fold_in(key, 11)
    second_key = jax.random.fold_in(key, 23)
    position = jnp.arange(D, dtype=jnp.float32) / D
    token_scale = jnp.exp(jax.random.uniform(second_key, (LENGTH, 1), minval=-0.7, maxval=0.7))
    basic = jnp.clip(jax.random.normal(first_key, (LENGTH, D)), -6.0, 6.0)
    channel_scale = 10.0 ** (position - 0.5)
    return (basic * token_scale * channel_scale[None, :]).astype(jnp.bfloat16)


def level_of(key, dims, cuts, smallest, high):
    factor_of, own = 1.0, jax.random.fold_in(key, 6)
    for axis_at, parts in cuts:
        heights = jnp.exp(jax.random.uniform(jax.random.fold_in(own, axis_at), (parts,), jnp.float32, smallest / len(cuts), high / len(cuts)))
        factor_of = factor_of * jnp.repeat(heights, dims[axis_at] // parts).reshape([-1 if axis == axis_at else 1 for axis in range(len(dims))])
    return factor_of


def gaussian(stream_key, extent, scale, bound, cuts=(), kind=jnp.bfloat16):
    values = scale * jax.random.normal(stream_key, extent, jnp.float32)
    if cuts:
        values = values * level_of(stream_key, extent, cuts, -0.22, 0.18)
    return jnp.clip(values, -bound, bound).astype(kind)


def setup_inputs(seed: int = 0) -> dict:
    splits = jax.random.split(jax.random.key(seed), 6)
    return {
        "queries": gaussian(splits[0], (LENGTH, D), 1.0, 6.0, ((0, 64), (1, 8))),
        "key_feats": gaussian(splits[1], (LENGTH, D), 1.0, 6.0, ((0, 64), (1, 8))),
        "value_feats": gaussian(splits[2], (LENGTH, D), 1.0, 6.0, ((0, 64), (1, 8))),
        "filters": gaussian(splits[3], (GROUPS, K), K ** -0.5, 0.5, ((0, 8),)),
        "grad_out": draw_grad_out(jax.random.fold_in(splits[5], 71), 0),
    }


def contract(formula, first_op, second_op):
    return jnp.einsum(formula, first_op.astype(jnp.float32), second_op.astype(jnp.float32), precision=lax.Precision.HIGHEST)

def toeplitz(filt):
    count, filter_len = filt.shape
    flipped = filt[:, ::-1]
    lead_zero = jnp.zeros((count, 1), filt.dtype)
    trailing = jnp.zeros((count, filter_len), filt.dtype)
    pattern = jnp.concatenate([lead_zero, flipped, trailing], axis=1)
    repeated = jnp.tile(pattern, (1, filter_len))
    return repeated[:, :filter_len * 2 * filter_len].reshape(count, filter_len, 2 * filter_len)

def make_windows(blocks, before):
    earlier = jnp.concatenate([before[:, :, None, :], blocks[:, :, :-1, :]], axis=2)
    return jnp.concatenate([earlier, blocks], axis=3)

def forward_conv(signal, before, toeplitz_mat):
    groups_here, group_size, seq_len = signal.shape
    filter_len = toeplitz_mat.shape[1]
    blocks = signal.reshape(groups_here, group_size, seq_len // filter_len, filter_len)
    window_rows = make_windows(blocks, before)
    result = contract('gam,gsnm->gsna', toeplitz_mat, window_rows)
    return (result.reshape(groups_here, group_size, seq_len), window_rows)

def backward_conv(grad_rows, after, toeplitz_mat):
    groups_here, group_size, seq_len = grad_rows.shape
    filter_len = toeplitz_mat.shape[1]
    blocks = grad_rows.reshape(groups_here, group_size, seq_len // filter_len, filter_len)
    spread = contract('gam,gsna->gsnm', toeplitz_mat, blocks)
    tail_part = contract('gam,gsa->gsm', toeplitz_mat, after)
    next_part = jnp.concatenate([spread[:, :, 1:, :filter_len], tail_part[:, :, None, :filter_len]], axis=2)
    return (spread[:, :, :, filter_len:] + next_part).reshape(groups_here, group_size, seq_len)

def filter_grad(grad_rows, window_rows, filter_len):
    groups_here, group_size, seq_len = grad_rows.shape
    blocks = grad_rows.reshape(groups_here, group_size, seq_len // filter_len, filter_len)
    correlate = contract('gsna,gsnm->gam', blocks, window_rows)
    flattened = correlate.reshape(groups_here, filter_len * 2 * filter_len)
    flattened = jnp.concatenate([flattened, jnp.zeros((groups_here, filter_len), jnp.float32)], axis=1)
    flattened = flattened.reshape(groups_here, filter_len, 2 * filter_len + 1)
    diagonals = lax.optimization_barrier(jnp.sum(flattened, axis=1))
    return diagonals[:, 1:filter_len + 1][:, ::-1]

def reference(queries, key_feats, value_feats, filters, grad_out):
    seq_len, channels = queries.shape
    slab_width = 1024
    slab_groups = slab_width // G
    outs_mixer, outs_query, outs_key, outs_value, outs_filter = ([], [], [], [], [])
    for slab_index in range(channels // slab_width):
        lower = slab_index * slab_width
        query_f = queries[:, lower:lower + slab_width].astype(jnp.float32)
        key_f = key_feats[:, lower:lower + slab_width].astype(jnp.float32)
        value_f = value_feats[:, lower:lower + slab_width].astype(jnp.float32)
        cot_f = grad_out[:, lower:lower + slab_width].astype(jnp.float32)
        own_filters = filters[slab_index * slab_groups:(slab_index + 1) * slab_groups]
        product = (key_f * value_f).astype(jnp.bfloat16)
        grad_mix = (cot_f * query_f).astype(jnp.bfloat16)
        signal = product.T.reshape(slab_groups, G, seq_len)
        grad_rows = grad_mix.T.reshape(slab_groups, G, seq_len)
        zero_rim = jnp.zeros((slab_groups, G, K), jnp.bfloat16)
        toeplitz_mat = toeplitz(own_filters)
        conv_out, window_rows = forward_conv(signal, zero_rim, toeplitz_mat)
        conv_out = conv_out.astype(jnp.bfloat16)
        conv_grad = backward_conv(grad_rows, zero_rim, toeplitz_mat).astype(jnp.bfloat16)
        outs_filter.append(filter_grad(grad_rows, window_rows, K))
        conv_f = conv_out.reshape(slab_width, seq_len).T.astype(jnp.float32)
        back_f = conv_grad.reshape(slab_width, seq_len).T.astype(jnp.float32)
        outs_mixer.append((query_f * conv_f).astype(jnp.bfloat16))
        outs_query.append((cot_f * conv_f).astype(jnp.bfloat16))
        outs_key.append((back_f * value_f).astype(jnp.bfloat16))
        outs_value.append((back_f * key_f).astype(jnp.bfloat16))
    raw_filters = jnp.concatenate(outs_filter, axis=0)
    grad_rms = jnp.sqrt(jnp.mean(raw_filters * raw_filters) + 1e-06)
    grad_filters = raw_filters * jnp.minimum(1.0, 1.0 / grad_rms)
    return (jnp.concatenate(outs_mixer, axis=1), jnp.concatenate(outs_query, axis=1), jnp.concatenate(outs_key, axis=1), jnp.concatenate(outs_value, axis=1), grad_filters)
```

```python
import jax
import jax.numpy as jnp
from jax import lax
from jax.experimental import pallas as pl
from jax.experimental.pallas import tpu as pltpu
from jax.sharding import Mesh, PartitionSpec as P

D = 8192
G = 16
K = 128
B = 64
W = 2 * K
LANES = 128
TILE_GROUPS = LANES // G
CTX = ("y", "zl", "x")
MP = ("zh", "core")


def gate(first_ref, second_ref):
    first = first_ref[...].astype(jnp.float32)
    return (first * second_ref[...].astype(jnp.float32)).astype(jnp.bfloat16)


def windows(rows, blocks):
    return jnp.concatenate([rows[n * B : n * B + W] for n in range(blocks)], axis=1)


def group_of_lane(shape):
    return (lax.broadcasted_iota(jnp.int32, shape, 1) % LANES) // G


def filter_kernel(q_ref, k_ref, v_ref, go_ref, after_ref, raw_ref):
    product = gate(k_ref, v_ref)
    mix = gate(go_ref, q_ref)
    blocks = product.shape[0] // B
    rows = jnp.concatenate([mix, after_ref[...], jnp.zeros((W - K - B, LANES), jnp.bfloat16)], axis=0)
    wins = windows(rows, blocks)
    left = jnp.concatenate([product[n * B : (n + 1) * B] for n in range(blocks)], axis=1)
    group = group_of_lane(left.shape)
    zero = jnp.zeros_like(left)
    left = jnp.concatenate([jnp.where(group == g, left, zero) for g in range(TILE_GROUPS)], axis=0)
    pairs = lax.dot_general(left, wins, (((1,), (1,)), ((), ())), preferred_element_type=jnp.float32)
    sub = lax.broadcasted_iota(jnp.int32, (8, W), 0)
    for g in range(TILE_GROUPS):
        total = pairs[g * B : g * B + 8]
        for r in range(1, B // 8):
            total = total + pltpu.roll(pairs[g * B + 8 * r : g * B + 8 * r + 8], W - 8 * r, 1)
        for bit in (1, 2, 4):
            total = jnp.where((sub & bit) != 0, pltpu.roll(total, W - bit, 1), total)
        raw_ref[g : g + 1, :] = jnp.sum(total[:, :K], axis=0, keepdims=True)


def toeplitz_rows(rows_ref):
    mats = []
    for g in range(TILE_GROUPS):
        row = jnp.broadcast_to(rows_ref[g : g + 1, :], (B, W))
        mats.append(pltpu.roll(row, 0, 1, stride=1, stride_axis=0).astype(jnp.bfloat16))
    return jnp.concatenate(mats, axis=0)


def convolve(rows_ref, rows, blocks):
    full = jnp.dot(toeplitz_rows(rows_ref), windows(rows, blocks), preferred_element_type=jnp.float32)
    group = group_of_lane((B, blocks * LANES))
    total = full[:B]
    for g in range(1, TILE_GROUPS):
        total = jnp.where(group == g, full[g * B : (g + 1) * B], total)
    total = total.astype(jnp.bfloat16).astype(jnp.float32)
    return jnp.concatenate([total[:, n * LANES : (n + 1) * LANES] for n in range(blocks)], axis=0)


def conv_kernel(
    q_ref, k_ref, v_ref, go_ref, before_ref, after_ref, forward_ref, backward_ref, mo_ref, gq_ref, gk_ref, gv_ref
):
    product = gate(k_ref, v_ref)
    mix = gate(go_ref, q_ref)
    blocks = product.shape[0] // B
    pad = jnp.zeros((W - K - B, LANES), jnp.bfloat16)
    out = convolve(forward_ref, jnp.concatenate([before_ref[...], product, pad], axis=0), blocks)
    mo_ref[...] = (q_ref[...].astype(jnp.float32) * out).astype(jnp.bfloat16)
    gq_ref[...] = (go_ref[...].astype(jnp.float32) * out).astype(jnp.bfloat16)
    back = convolve(backward_ref, jnp.concatenate([mix, after_ref[...], pad], axis=0), blocks)
    gk_ref[...] = (back * v_ref[...].astype(jnp.float32)).astype(jnp.bfloat16)
    gv_ref[...] = (back * k_ref[...].astype(jnp.float32)).astype(jnp.bfloat16)


def product_of(first, second):
    return (first.astype(jnp.float32) * second.astype(jnp.float32)).astype(jnp.bfloat16)


def sum_over(value, axes):
    size = lax.axis_size(axes)
    spread = jnp.broadcast_to(value[None], (size,) + value.shape)
    return jnp.sum(lax.all_to_all(spread, axes, split_axis=0, concat_axis=0, tiled=True), axis=0)


def shards(queries, key_feats, value_feats, filters, grad_out):
    tokens, channels = queries.shape
    slab_groups = filters.shape[0]
    owners = lax.axis_size(CTX)
    tail = product_of(key_feats[tokens - K :], value_feats[tokens - K :])
    head = product_of(grad_out[:K], queries[:K])
    after = lax.ppermute(head, CTX, [(i + 1, i) for i in range(owners - 1)])
    before = lax.ppermute(tail, CTX, [(i, i + 1) for i in range(owners - 1)])

    tiles = channels // LANES
    whole = pl.BlockSpec((tokens, LANES), lambda i: (0, i))
    halo = pl.BlockSpec((K, LANES), lambda i: (0, i))
    group_rows = pl.BlockSpec((TILE_GROUPS, W), lambda i: (i, 0))
    raw = pl.pallas_call(
        filter_kernel,
        grid=(tiles,),
        in_specs=[whole] * 4 + [halo],
        out_specs=pl.BlockSpec((TILE_GROUPS, K), lambda i: (i, 0)),
        out_shape=jax.ShapeDtypeStruct((slab_groups, K), jnp.float32),
        cost_estimate=pl.CostEstimate(flops=10**9, bytes_accessed=5 * 2**19, transcendentals=0),
        name="filter_grad",
    )(queries, key_feats, value_feats, grad_out, after)

    filt = filters.astype(jnp.float32)
    zeros = jnp.zeros((slab_groups, W - K), jnp.float32)
    backward_rows = jnp.concatenate([filt, zeros], axis=1)
    forward_rows = jnp.concatenate([zeros[:, :1], filt[:, ::-1], zeros[:, 1:]], axis=1)
    wide = jax.ShapeDtypeStruct((tokens, channels), jnp.bfloat16)
    mixer_out, grad_queries, grad_keys, grad_values = pl.pallas_call(
        conv_kernel,
        grid=(tiles,),
        in_specs=[whole] * 4 + [halo] * 2 + [group_rows] * 2,
        out_specs=[whole] * 4,
        out_shape=[wide] * 4,
        cost_estimate=pl.CostEstimate(flops=2 * 10**9, bytes_accessed=9 * 2**19, transcendentals=0),
        name="conv",
    )(queries, key_feats, value_feats, grad_out, before, after, forward_rows, backward_rows)

    raw = sum_over(raw, ("zl", "x"))
    raw = sum_over(raw, ("y",))
    squares = sum_over(jnp.sum(raw * raw, axis=0, keepdims=True), MP)
    grad_rms = jnp.sqrt(jnp.sum(squares) / (D // G * K) + 1e-06)
    grad_filters = raw * jnp.minimum(1.0, 1.0 / grad_rms)
    return (mixer_out, grad_queries, grad_keys, grad_values, grad_filters)


def solution(mesh):
    fine = Mesh(mesh.devices.reshape(8, 2, 4, 4, 2), CTX + MP)
    placed = (P(CTX, MP), P(CTX, MP), P(CTX, MP), P(MP, None), P(CTX, MP))
    return jax.shard_map(
        shards,
        mesh=fine,
        in_specs=placed,
        out_specs=(P(CTX, MP), P(CTX, MP), P(CTX, MP), P(CTX, MP), P(MP, None)),
        check_vma=False,
    )
```

```python
import functools

import jax
import jax.numpy as jnp
from jax import lax
from jax.experimental import pallas as pl
from jax.experimental.pallas import tpu as pltpu
from jax.sharding import Mesh, PartitionSpec as P

D = 8192
G = 16
K = 128
B = 32
FB = 32
W = 2 * K
LANES = 128
UNROLL = 4
TILE_GROUPS = LANES // G
CTX = ("y", "zl", "x")
MP = ("zh", "core")
HBM = pl.BlockSpec(memory_space=pl.ANY)
VMEM = pl.BlockSpec(memory_space=pltpu.VMEM)


def product_of(first, second):
    return (first.astype(jnp.float32) * second.astype(jnp.float32)).astype(jnp.bfloat16)


def blocks_of(rows, size):
    return jnp.concatenate([rows[n : n + size] for n in range(0, rows.shape[0], size)], axis=1)


def windows(rows, size):
    return jnp.concatenate([rows[n : n + W] for n in range(0, rows.shape[0] - W + size, size)], axis=1)


def group_of_lane(shape):
    return (lax.broadcasted_iota(jnp.int32, shape, 1) % LANES) // G


def correlate(product, following, tile, rows_ref):
    left = blocks_of(product, FB)
    group = group_of_lane(left.shape)
    zero = jnp.zeros_like(left)
    left = jnp.concatenate([jnp.where(group == g, left, zero) for g in range(TILE_GROUPS)], axis=0)
    pad = jnp.zeros((product.shape[0] - FB + W - following.shape[0], LANES), jnp.bfloat16)
    wins = windows(jnp.concatenate([following, pad], axis=0), FB)
    pairs = lax.dot_general(left, wins, (((1,), (1,)), ((), ())), preferred_element_type=jnp.float32)
    for g in range(TILE_GROUPS):
        total = pairs[g * FB : g * FB + 8]
        for r in range(8, FB, 8):
            total = total + pltpu.roll(pairs[g * FB + r : g * FB + r + 8], W - r, 1)
        rows_ref[pl.ds((tile * TILE_GROUPS + g) * 8, 8), :] = total


def fold(rows_ref):
    rows = rows_ref[...]
    sub = lax.broadcasted_iota(jnp.int32, rows.shape, 0)
    for bit in (1, 2, 4):
        rows = jnp.where((sub & bit) != 0, pltpu.roll(rows, W - bit, 1), rows)
    return jnp.sum(rows[:, :K].reshape(rows.shape[0] // 8, 8, K), axis=1)


def lanes_of(tile):
    return pl.ds(pl.multiple_of(tile * LANES, LANES), LANES)


def copies_of(pairs, tile, sems):
    c = lanes_of(tile)
    return [pltpu.make_async_copy(src.at[:, c], dst.at[:, c], sems.at[n, tile]) for n, (src, dst) in enumerate(pairs)]


def start_all(pairs, tiles, sems):
    @pl.loop(0, tiles)
    def _(t):
        for copy in copies_of(pairs, t, sems):
            copy.start()


def local_kernel(q_hbm, k_hbm, v_hbm, go_hbm, raw_ref, q_buf, k_buf, v_buf, go_buf, rows, sems):
    pairs = ((k_hbm, k_buf), (v_hbm, v_buf), (go_hbm, go_buf), (q_hbm, q_buf))
    tiles = q_buf.shape[1] // LANES
    start_all(pairs, tiles, sems)

    @pl.loop(0, tiles, unroll=2)
    def _(t):
        c = lanes_of(t)
        for copy in copies_of(pairs, t, sems):
            copy.wait()
        correlate(product_of(k_buf[:, c], v_buf[:, c]), product_of(go_buf[:, c], q_buf[:, c]), t, rows)

    raw_ref[...] = fold(rows)


def edge_kernel(tail_ref, after_ref, local_ref, raw_ref, rows):
    @pl.loop(0, tail_ref.shape[1] // LANES, unroll=UNROLL)
    def _(t):
        c = lanes_of(t)
        following = jnp.concatenate([jnp.zeros((K, LANES), jnp.bfloat16), after_ref[:, c]], axis=0)
        correlate(tail_ref[:, c], following, t, rows)

    raw_ref[...] = local_ref[...] + fold(rows)


def toeplitz_rows(rows_ref, t):
    mats = []
    for g in range(TILE_GROUPS):
        row = jnp.broadcast_to(rows_ref[pl.ds(t * TILE_GROUPS + g, 1), :], (B, W))
        mats.append(pltpu.roll(row, 0, 1, stride=1, stride_axis=0).astype(jnp.bfloat16))
    return jnp.concatenate(mats, axis=0)


def convolve(mats, rows):
    blocks = (rows.shape[0] - K) // B
    pad = jnp.zeros((W - K - B, LANES), jnp.bfloat16)
    wins = windows(jnp.concatenate([rows, pad], axis=0), B)
    full = jnp.dot(mats, wins, preferred_element_type=jnp.float32)
    group = group_of_lane((B, blocks * LANES))
    total = full[:B]
    for g in range(1, TILE_GROUPS):
        total = jnp.where(group == g, full[g * B : (g + 1) * B], total)
    total = total.astype(jnp.bfloat16).astype(jnp.float32)
    return jnp.concatenate([total[:, n * LANES : (n + 1) * LANES] for n in range(blocks)], axis=0)


def conv_kernel(
    causal, a_hbm, b_hbm, x_hbm, y_hbm, halo_ref, filter_ref, ox_hbm, oy_hbm,
    a_buf, b_buf, x_buf, y_buf, ox_buf, oy_buf, in_sems, out_sems,
):
    tiles = a_buf.shape[1] // LANES
    ins = ((a_hbm, a_buf), (b_hbm, b_buf), (x_hbm, x_buf), (y_hbm, y_buf))
    outs = ((ox_buf, ox_hbm), (oy_buf, oy_hbm))
    start_all(ins, tiles, in_sems)

    @pl.loop(0, tiles, unroll=2)
    def _(t):
        c = lanes_of(t)
        mats = toeplitz_rows(filter_ref, t)
        for copy in copies_of(ins, t, in_sems):
            copy.wait()
        own, halo = product_of(a_buf[:, c], b_buf[:, c]), halo_ref[:, c]
        out = convolve(mats, jnp.concatenate([halo, own] if causal else [own, halo], axis=0))
        ox_buf[:, c] = (out * x_buf[:, c].astype(jnp.float32)).astype(jnp.bfloat16)
        oy_buf[:, c] = (out * y_buf[:, c].astype(jnp.float32)).astype(jnp.bfloat16)
        for copy in copies_of(outs, t, out_sems):
            copy.start()

    @pl.loop(0, tiles)
    def _(t):
        for copy in copies_of(outs, t, out_sems):
            copy.wait()


def local_filter(q, k, v, go, slab_groups):
    tokens, channels = q.shape
    return pl.pallas_call(
        local_kernel,
        in_specs=[HBM] * 4,
        out_specs=VMEM,
        out_shape=jax.ShapeDtypeStruct((slab_groups, K), jnp.float32),
        scratch_shapes=[pltpu.VMEM((tokens, channels), jnp.bfloat16)] * 4
        + [pltpu.VMEM((slab_groups * 8, W), jnp.float32), pltpu.SemaphoreType.DMA((4, channels // LANES))],
        cost_estimate=pl.CostEstimate(flops=3 * 10**9, bytes_accessed=2**21, transcendentals=0),
        compiler_params=pltpu.CompilerParams(vmem_limit_bytes=8 << 20),
        name="local_filter",
    )(q, k, v, go)


def edge_filter(tail, after, local):
    return pl.pallas_call(
        edge_kernel,
        in_specs=[VMEM] * 3,
        out_specs=VMEM,
        out_shape=jax.ShapeDtypeStruct(local.shape, jnp.float32),
        scratch_shapes=[pltpu.VMEM((local.shape[0] * 8, W), jnp.float32)],
        cost_estimate=pl.CostEstimate(flops=10**9, bytes_accessed=2**19, transcendentals=0),
        compiler_params=pltpu.CompilerParams(vmem_limit_bytes=4 << 20),
        name="edge_filter",
    )(tail, after, local)


def conv(causal, signal, factors, halo, filter_rows):
    wide = jax.ShapeDtypeStruct(signal[0].shape, jnp.bfloat16)
    buffer = pltpu.VMEM(wide.shape, jnp.bfloat16)
    sems = [pltpu.SemaphoreType.DMA((n, wide.shape[1] // LANES)) for n in (4, 2)]
    return pl.pallas_call(
        functools.partial(conv_kernel, causal),
        in_specs=[HBM] * 4 + [VMEM] * 2,
        out_specs=[HBM] * 2,
        out_shape=[wide] * 2,
        scratch_shapes=[buffer] * 6 + sems,
        cost_estimate=pl.CostEstimate(flops=2 * 10**9, bytes_accessed=3 * 2**20, transcendentals=0),
        compiler_params=pltpu.CompilerParams(vmem_limit_bytes=10 << 20),
        name="forward_conv" if causal else "backward_conv",
    )(*signal, *factors, halo, filter_rows)


def sum_over(value, axes):
    size = lax.axis_size(axes)
    spread = jnp.broadcast_to(value[None], (size,) + value.shape)
    return jnp.sum(lax.all_to_all(spread, axes, split_axis=0, concat_axis=0, tiled=True), axis=0)


def shards(queries, key_feats, value_feats, filters, grad_out):
    tokens = queries.shape[0]
    slab_groups = filters.shape[0]
    owners = lax.axis_size(CTX)
    head = product_of(grad_out[:K], queries[:K])
    after = lax.ppermute(head, CTX, [(i + 1, i) for i in range(owners - 1)])
    tail = product_of(key_feats[tokens - K :], value_feats[tokens - K :])
    before = lax.ppermute(tail, CTX, [(i, i + 1) for i in range(owners - 1)])

    local = local_filter(queries, key_feats, value_feats, grad_out, slab_groups)
    raw = edge_filter(tail, after, local)

    filt = filters.astype(jnp.float32)
    zeros = jnp.zeros((slab_groups, W - K), jnp.float32)
    backward_rows = jnp.concatenate([filt, zeros], axis=1)
    forward_rows = jnp.concatenate([zeros[:, :1], filt[:, ::-1], zeros[:, 1:]], axis=1)

    raw, before = lax.optimization_barrier((raw, before))
    forward = conv(True, (key_feats, value_feats), (queries, grad_out), before, forward_rows)
    raw = sum_over(raw, ("zl", "x"))
    raw, after, forward = lax.optimization_barrier((raw, after, forward))
    backward = conv(False, (grad_out, queries), (value_feats, key_feats), after, backward_rows)
    raw = sum_over(raw, ("y",))
    raw, backward = lax.optimization_barrier((raw, backward))
    squares = sum_over(jnp.sum(raw * raw, axis=0, keepdims=True), MP)
    grad_rms = jnp.sqrt(jnp.sum(squares) / (D // G * K) + 1e-06)
    grad_filters = raw * jnp.minimum(1.0, 1.0 / grad_rms)
    return (*forward, *backward, grad_filters)


def solution(mesh):
    fine = Mesh(mesh.devices.reshape(8, 2, 4, 4, 2), CTX + MP)
    placed = (P(CTX, MP), P(CTX, MP), P(CTX, MP), P(MP, None), P(CTX, MP))
    return jax.shard_map(
        shards,
        mesh=fine,
        in_specs=placed,
        out_specs=(P(CTX, MP), P(CTX, MP), P(CTX, MP), P(CTX, MP), P(MP, None)),
        check_vma=False,
    )
```

```python
import functools

import jax
import jax.numpy as jnp
from jax import lax
from jax.experimental import pallas as pl
from jax.experimental.pallas import tpu as pltpu
from jax.sharding import Mesh, PartitionSpec as P

D = 8192
G = 16
K = 128
B = 16
FB = 32
W = 2 * K
LANES = 128
UNROLL = 4
LIMIT = 8 << 20
TILE_GROUPS = LANES // G
CTX = ("y", "zl", "x")
MP = ("zh", "core")
HBM = pl.BlockSpec(memory_space=pl.ANY)
VMEM = pl.BlockSpec(memory_space=pltpu.VMEM)


def product_of(first, second):
    return (first.astype(jnp.float32) * second.astype(jnp.float32)).astype(jnp.bfloat16)


def blocks_of(rows, size):
    return jnp.concatenate([rows[n : n + size] for n in range(0, rows.shape[0], size)], axis=1)


def windows(rows, size):
    return jnp.concatenate([rows[n : n + W] for n in range(0, rows.shape[0] - W + size, size)], axis=1)


def group_of_lane(shape):
    return (lax.broadcasted_iota(jnp.int32, shape, 1) % LANES) // G


def correlate(product, following, tile, rows_ref):
    left = blocks_of(product, FB)
    group = group_of_lane(left.shape)
    zero = jnp.zeros_like(left)
    left = jnp.concatenate([jnp.where(group == g, left, zero) for g in range(TILE_GROUPS)], axis=0)
    pad = jnp.zeros((product.shape[0] - FB + W - following.shape[0], LANES), jnp.bfloat16)
    wins = windows(jnp.concatenate([following, pad], axis=0), FB)
    pairs = lax.dot_general(left, wins, (((1,), (1,)), ((), ())), preferred_element_type=jnp.float32)
    for g in range(TILE_GROUPS):
        total = pairs[g * FB : g * FB + 8]
        for r in range(8, FB, 8):
            total = total + pltpu.roll(pairs[g * FB + r : g * FB + r + 8], W - r, 1)
        rows_ref[pl.ds((tile * TILE_GROUPS + g) * 8, 8), :] = total


def fold(rows_ref):
    rows = rows_ref[...]
    sub = lax.broadcasted_iota(jnp.int32, rows.shape, 0)
    for bit in (1, 2, 4):
        rows = jnp.where((sub & bit) != 0, pltpu.roll(rows, W - bit, 1), rows)
    return jnp.sum(rows[:, :K].reshape(rows.shape[0] // 8, 8, K), axis=1)


def lanes_of(tile):
    return pl.ds(pl.multiple_of(tile * LANES, LANES), LANES)


def local_kernel(q_ref, k_ref, v_ref, go_ref, raw_ref, tail_ref, rows):
    tokens = q_ref.shape[0]

    @pl.loop(0, q_ref.shape[1] // LANES, unroll=UNROLL)
    def _(t):
        c = lanes_of(t)
        product = product_of(k_ref[:, c], v_ref[:, c])
        tail_ref[:, c] = product[tokens - K :]
        correlate(product, product_of(go_ref[:, c], q_ref[:, c]), t, rows)

    raw_ref[...] = fold(rows)


def edge_kernel(tail_ref, after_ref, local_ref, raw_ref, rows):
    @pl.loop(0, tail_ref.shape[1] // LANES, unroll=UNROLL)
    def _(t):
        c = lanes_of(t)
        following = jnp.concatenate([jnp.zeros((K, LANES), jnp.bfloat16), after_ref[:, c]], axis=0)
        correlate(tail_ref[:, c], following, t, rows)

    raw_ref[...] = local_ref[...] + fold(rows)


def scale_kernel(raw_ref, squares_ref, out_ref):
    raw = raw_ref[...]
    mean = jnp.sum(squares_ref[...], axis=(0, 1), keepdims=True)[0]
    mean = jnp.sum(mean, axis=1, keepdims=True) / (D // G * K)
    out_ref[...] = raw * jnp.minimum(1.0, 1.0 / jnp.sqrt(mean + 1e-06))


def toeplitz_rows(rows_ref, t):
    mats = []
    for g in range(TILE_GROUPS):
        row = jnp.broadcast_to(rows_ref[pl.ds(t * TILE_GROUPS + g, 1), :], (B, W))
        mats.append(pltpu.roll(row, 0, 1, stride=1, stride_axis=0).astype(jnp.bfloat16))
    return jnp.concatenate(mats, axis=0)


def convolve(mats, rows):
    blocks = (rows.shape[0] - K) // B
    pad = jnp.zeros((W - K - B, LANES), jnp.bfloat16)
    wins = windows(jnp.concatenate([rows, pad], axis=0), B)
    full = jnp.dot(mats, wins, preferred_element_type=jnp.float32)
    group = group_of_lane((B, blocks * LANES))
    total = full[:B]
    for g in range(1, TILE_GROUPS):
        total = jnp.where(group == g, full[g * B : (g + 1) * B], total)
    total = total.astype(jnp.bfloat16).astype(jnp.float32)
    return jnp.concatenate([total[:, n * LANES : (n + 1) * LANES] for n in range(blocks)], axis=0)


def conv_kernel(causal, a_ref, b_ref, x_ref, y_ref, halo_ref, filter_ref, ox_hbm, oy_hbm, ox_buf, oy_buf, sems):
    tiles = a_ref.shape[1] // LANES

    def copies_of(t):
        c = lanes_of(t)
        pairs = ((ox_buf, ox_hbm), (oy_buf, oy_hbm))
        return [pltpu.make_async_copy(src.at[:, c], dst.at[:, c], sems.at[n, t]) for n, (src, dst) in enumerate(pairs)]

    @pl.loop(0, tiles, unroll=2)
    def _(t):
        c = lanes_of(t)
        own, halo = product_of(a_ref[:, c], b_ref[:, c]), halo_ref[:, c]
        out = convolve(toeplitz_rows(filter_ref, t), jnp.concatenate([halo, own] if causal else [own, halo], axis=0))
        ox_buf[:, c] = (out * x_ref[:, c].astype(jnp.float32)).astype(jnp.bfloat16)
        oy_buf[:, c] = (out * y_ref[:, c].astype(jnp.float32)).astype(jnp.bfloat16)
        for copy in copies_of(t):
            copy.start()

    @pl.loop(0, tiles)
    def _(t):
        for copy in copies_of(t):
            copy.wait()


def local_filter(q, k, v, go, slab_groups):
    return pl.pallas_call(
        local_kernel,
        in_specs=[VMEM] * 4,
        out_specs=[VMEM] * 2,
        out_shape=[
            jax.ShapeDtypeStruct((slab_groups, K), jnp.float32),
            jax.ShapeDtypeStruct((K, q.shape[1]), jnp.bfloat16),
        ],
        scratch_shapes=[pltpu.VMEM((slab_groups * 8, W), jnp.float32)],
        cost_estimate=pl.CostEstimate(flops=3 * 10**9, bytes_accessed=2**21, transcendentals=0),
        compiler_params=pltpu.CompilerParams(vmem_limit_bytes=LIMIT),
        name="local_filter",
    )(q, k, v, go)


def edge_filter(tail, after, local):
    return pl.pallas_call(
        edge_kernel,
        in_specs=[VMEM] * 3,
        out_specs=VMEM,
        out_shape=jax.ShapeDtypeStruct(local.shape, jnp.float32),
        scratch_shapes=[pltpu.VMEM((local.shape[0] * 8, W), jnp.float32)],
        cost_estimate=pl.CostEstimate(flops=10**9, bytes_accessed=2**19, transcendentals=0),
        compiler_params=pltpu.CompilerParams(vmem_limit_bytes=LIMIT),
        name="edge_filter",
    )(tail, after, local)


def conv(causal, signal, factors, halo, filter_rows):
    wide = jax.ShapeDtypeStruct(signal[0].shape, jnp.bfloat16)
    return pl.pallas_call(
        functools.partial(conv_kernel, causal),
        in_specs=[VMEM] * 6,
        out_specs=[HBM] * 2,
        out_shape=[wide] * 2,
        scratch_shapes=[pltpu.VMEM(wide.shape, jnp.bfloat16)] * 2
        + [pltpu.SemaphoreType.DMA((2, wide.shape[1] // LANES))],
        cost_estimate=pl.CostEstimate(flops=2 * 10**9, bytes_accessed=3 * 2**20, transcendentals=0),
        compiler_params=pltpu.CompilerParams(vmem_limit_bytes=LIMIT),
        name="forward_conv" if causal else "backward_conv",
    )(*signal, *factors, halo, filter_rows)


def scale(raw, squares):
    return pl.pallas_call(
        scale_kernel,
        in_specs=[VMEM] * 2,
        out_specs=VMEM,
        out_shape=jax.ShapeDtypeStruct(raw.shape, jnp.float32),
        compiler_params=pltpu.CompilerParams(vmem_limit_bytes=LIMIT),
        name="scale",
    )(raw, squares)


def spread_over(value, axes):
    size = lax.axis_size(axes)
    spread = jnp.broadcast_to(value[None], (size,) + value.shape)
    return lax.all_to_all(spread, axes, split_axis=0, concat_axis=0, tiled=True)


def shards(queries, key_feats, value_feats, filters, grad_out):
    slab_groups = filters.shape[0]
    owners = lax.axis_size(CTX)
    head = product_of(grad_out[:K], queries[:K])
    after = lax.ppermute(head, CTX, [(i + 1, i) for i in range(owners - 1)])
    local, tail = local_filter(queries, key_feats, value_feats, grad_out, slab_groups)
    raw = edge_filter(tail, after, local)

    filt = filters.astype(jnp.float32)
    zeros = jnp.zeros((slab_groups, W - K), jnp.float32)
    backward_rows = jnp.concatenate([filt, zeros], axis=1)
    forward_rows = jnp.concatenate([zeros[:, :1], filt[:, ::-1], zeros[:, 1:]], axis=1)

    raw, tail, after = lax.optimization_barrier((raw, tail, after))
    before = lax.ppermute(tail, CTX, [(i, i + 1) for i in range(owners - 1)])
    backward = conv(False, (grad_out, queries), (value_feats, key_feats), after, backward_rows)
    raw = jnp.sum(spread_over(raw, ("zl", "x")), axis=0)
    raw, before, backward = lax.optimization_barrier((raw, before, backward))
    forward = conv(True, (key_feats, value_feats), (queries, grad_out), before, forward_rows)
    raw = jnp.sum(spread_over(raw, ("y",)), axis=0)
    raw, forward = lax.optimization_barrier((raw, forward))
    grad_filters = scale(raw, spread_over(jnp.sum(raw * raw, axis=0, keepdims=True), MP))
    return (*forward, *backward, grad_filters)


def solution(mesh):
    fine = Mesh(mesh.devices.reshape(8, 2, 4, 4, 2), CTX + MP)
    placed = (P(CTX, MP), P(CTX, MP), P(CTX, MP), P(MP, None), P(CTX, MP))
    return jax.shard_map(
        shards,
        mesh=fine,
        in_specs=placed,
        out_specs=(P(CTX, MP), P(CTX, MP), P(CTX, MP), P(CTX, MP), P(MP, None)),
        check_vma=False,
    )
```

```python
import functools

import jax
import jax.numpy as jnp
from jax import lax
from jax.experimental import pallas as pl
from jax.experimental.pallas import tpu as pltpu
from jax.sharding import Mesh, PartitionSpec as P

D = 8192
G = 16
K = 128
B = 16
FB = 32
W = 2 * K
LANES = 128
UNROLL = 4
LIMIT = 8 << 20
TILE_GROUPS = LANES // G
CTX = ("y", "zl", "x")
MP = ("zh", "core")
HBM = pl.BlockSpec(memory_space=pl.ANY)
VMEM = pl.BlockSpec(memory_space=pltpu.VMEM)


def product_of(first, second):
    return (first.astype(jnp.float32) * second.astype(jnp.float32)).astype(jnp.bfloat16)


def blocks_of(rows, size):
    return jnp.concatenate([rows[n : n + size] for n in range(0, rows.shape[0], size)], axis=1)


def windows(rows, size):
    return jnp.concatenate([rows[n : n + W] for n in range(0, rows.shape[0] - W + size, size)], axis=1)


def group_of_lane(shape):
    return (lax.broadcasted_iota(jnp.int32, shape, 1) % LANES) // G


def correlate(product, following, tile, rows_ref):
    left = blocks_of(product, FB)
    group = group_of_lane(left.shape)
    zero = jnp.zeros_like(left)
    left = jnp.concatenate([jnp.where(group == g, left, zero) for g in range(TILE_GROUPS)], axis=0)
    pad = jnp.zeros((product.shape[0] - FB + W - following.shape[0], LANES), jnp.bfloat16)
    wins = windows(jnp.concatenate([following, pad], axis=0), FB)
    pairs = lax.dot_general(left, wins, (((1,), (1,)), ((), ())), preferred_element_type=jnp.float32)
    for g in range(TILE_GROUPS):
        total = pairs[g * FB : g * FB + 8]
        for r in range(8, FB, 8):
            total = total + pltpu.roll(pairs[g * FB + r : g * FB + r + 8], W - r, 1)
        rows_ref[pl.ds((tile * TILE_GROUPS + g) * 8, 8), :] = total


def fold(rows_ref):
    rows = rows_ref[...]
    sub = lax.broadcasted_iota(jnp.int32, rows.shape, 0)
    for bit in (1, 2, 4):
        rows = jnp.where((sub & bit) != 0, pltpu.roll(rows, W - bit, 1), rows)
    return jnp.sum(rows[:, :K].reshape(rows.shape[0] // 8, 8, K), axis=1)


def lanes_of(tile):
    return pl.ds(pl.multiple_of(tile * LANES, LANES), LANES)


def local_kernel(q_ref, k_ref, v_ref, go_ref, raw_ref, tail_ref, rows):
    tokens = q_ref.shape[0]

    @pl.loop(0, q_ref.shape[1] // LANES, unroll=UNROLL)
    def _(t):
        c = lanes_of(t)
        product = product_of(k_ref[:, c], v_ref[:, c])
        tail_ref[:, c] = product[tokens - K :]
        correlate(product, product_of(go_ref[:, c], q_ref[:, c]), t, rows)

    raw_ref[...] = fold(rows)


def edge_kernel(tail_ref, after_ref, local_ref, raw_ref, rows):
    @pl.loop(0, tail_ref.shape[1] // LANES, unroll=UNROLL)
    def _(t):
        c = lanes_of(t)
        following = jnp.concatenate([jnp.zeros((K, LANES), jnp.bfloat16), after_ref[:, c]], axis=0)
        correlate(tail_ref[:, c], following, t, rows)

    raw_ref[...] = local_ref[...] + fold(rows)


def scale_kernel(raw_ref, squares_ref, out_ref):
    raw = raw_ref[...]
    mean = jnp.sum(squares_ref[...], axis=(0, 1), keepdims=True)[0]
    mean = jnp.sum(mean, axis=1, keepdims=True) / (D // G * K)
    out_ref[...] = raw * jnp.minimum(1.0, 1.0 / jnp.sqrt(mean + 1e-06))


def toeplitz_rows(rows_ref, t):
    mats = []
    for g in range(TILE_GROUPS):
        row = jnp.broadcast_to(rows_ref[pl.ds(t * TILE_GROUPS + g, 1), :], (B, W))
        mats.append(pltpu.roll(row, 0, 1, stride=1, stride_axis=0).astype(jnp.bfloat16))
    return jnp.concatenate(mats, axis=0)


def convolve(mats, rows):
    blocks = (rows.shape[0] - K) // B
    pad = jnp.zeros((W - K - B, LANES), jnp.bfloat16)
    wins = windows(jnp.concatenate([rows, pad], axis=0), B)
    full = jnp.dot(mats, wins, preferred_element_type=jnp.float32)
    group = group_of_lane((B, blocks * LANES))
    total = full[:B]
    for g in range(1, TILE_GROUPS):
        total = jnp.where(group == g, full[g * B : (g + 1) * B], total)
    total = total.astype(jnp.bfloat16).astype(jnp.float32)
    return jnp.concatenate([total[:, n * LANES : (n + 1) * LANES] for n in range(blocks)], axis=0)


def conv_kernel(causal, a_ref, b_ref, x_ref, y_ref, halo_ref, filter_ref, ox_hbm, oy_hbm, ox_buf, oy_buf, sems):
    tiles = a_ref.shape[1] // LANES

    def copies_of(t):
        c = lanes_of(t)
        pairs = ((ox_buf, ox_hbm), (oy_buf, oy_hbm))
        return [pltpu.make_async_copy(src.at[:, c], dst.at[:, c], sems.at[n, t]) for n, (src, dst) in enumerate(pairs)]

    @pl.loop(0, tiles, unroll=2)
    def _(t):
        c = lanes_of(t)
        own, halo = product_of(a_ref[:, c], b_ref[:, c]), halo_ref[:, c]
        out = convolve(toeplitz_rows(filter_ref, t), jnp.concatenate([halo, own] if causal else [own, halo], axis=0))
        ox_buf[:, c] = (out * x_ref[:, c].astype(jnp.float32)).astype(jnp.bfloat16)
        oy_buf[:, c] = (out * y_ref[:, c].astype(jnp.float32)).astype(jnp.bfloat16)
        for copy in copies_of(t):
            copy.start()

    @pl.loop(0, tiles)
    def _(t):
        for copy in copies_of(t):
            copy.wait()


def local_filter(q, k, v, go, slab_groups):
    return pl.pallas_call(
        local_kernel,
        in_specs=[VMEM] * 4,
        out_specs=[VMEM] * 2,
        out_shape=[
            jax.ShapeDtypeStruct((slab_groups, K), jnp.float32),
            jax.ShapeDtypeStruct((K, q.shape[1]), jnp.bfloat16),
        ],
        scratch_shapes=[pltpu.VMEM((slab_groups * 8, W), jnp.float32)],
        cost_estimate=pl.CostEstimate(flops=3 * 10**9, bytes_accessed=2**21, transcendentals=0),
        compiler_params=pltpu.CompilerParams(vmem_limit_bytes=LIMIT),
        name="local_filter",
    )(q, k, v, go)


def edge_filter(tail, after, local):
    return pl.pallas_call(
        edge_kernel,
        in_specs=[VMEM] * 3,
        out_specs=VMEM,
        out_shape=jax.ShapeDtypeStruct(local.shape, jnp.float32),
        scratch_shapes=[pltpu.VMEM((local.shape[0] * 8, W), jnp.float32)],
        cost_estimate=pl.CostEstimate(flops=10**9, bytes_accessed=2**19, transcendentals=0),
        compiler_params=pltpu.CompilerParams(vmem_limit_bytes=LIMIT),
        name="edge_filter",
    )(tail, after, local)


def conv(causal, signal, factors, halo, filter_rows):
    wide = jax.ShapeDtypeStruct(signal[0].shape, jnp.bfloat16)
    return pl.pallas_call(
        functools.partial(conv_kernel, causal),
        in_specs=[VMEM] * 6,
        out_specs=[HBM] * 2,
        out_shape=[wide] * 2,
        scratch_shapes=[pltpu.VMEM(wide.shape, jnp.bfloat16)] * 2
        + [pltpu.SemaphoreType.DMA((2, wide.shape[1] // LANES))],
        cost_estimate=pl.CostEstimate(flops=10**10, bytes_accessed=3 * 2**20, transcendentals=0),
        compiler_params=pltpu.CompilerParams(vmem_limit_bytes=LIMIT),
        name="forward_conv" if causal else "backward_conv",
    )(*signal, *factors, halo, filter_rows)


def scale(raw, squares):
    return pl.pallas_call(
        scale_kernel,
        in_specs=[VMEM] * 2,
        out_specs=VMEM,
        out_shape=jax.ShapeDtypeStruct(raw.shape, jnp.float32),
        compiler_params=pltpu.CompilerParams(vmem_limit_bytes=LIMIT),
        name="scale",
    )(raw, squares)


def spread_over(value, axes):
    size = lax.axis_size(axes)
    spread = jnp.broadcast_to(value[None], (size,) + value.shape)
    return lax.all_to_all(spread, axes, split_axis=0, concat_axis=0, tiled=True)


def shards(queries, key_feats, value_feats, filters, grad_out):
    slab_groups = filters.shape[0]
    owners = lax.axis_size(CTX)
    head = product_of(grad_out[:K], queries[:K])
    after = lax.ppermute(head, CTX, [(i + 1, i) for i in range(owners - 1)])
    local, tail = local_filter(queries, key_feats, value_feats, grad_out, slab_groups)
    raw = edge_filter(tail, after, local)

    filt = filters.astype(jnp.float32)
    zeros = jnp.zeros((slab_groups, W - K), jnp.float32)
    backward_rows = jnp.concatenate([filt, zeros], axis=1)
    forward_rows = jnp.concatenate([zeros[:, :1], filt[:, ::-1], zeros[:, 1:]], axis=1)

    before = lax.ppermute(tail, CTX, [(i, i + 1) for i in range(owners - 1)])
    before, after, _ = lax.optimization_barrier((before, after, raw))
    backward = conv(False, (grad_out, queries), (value_feats, key_feats), after, backward_rows)
    raw = jnp.sum(spread_over(raw, ("zl", "x")), axis=0)
    raw, backward = lax.optimization_barrier((raw, backward))
    before, _ = lax.optimization_barrier((before, raw))
    forward = conv(True, (key_feats, value_feats), (queries, grad_out), before, forward_rows)
    raw = jnp.sum(spread_over(raw, ("y",)), axis=0)
    raw, forward = lax.optimization_barrier((raw, forward))
    grad_filters = scale(raw, spread_over(jnp.sum(raw * raw, axis=0, keepdims=True), MP))
    return (*forward, *backward, grad_filters)


def solution(mesh):
    fine = Mesh(mesh.devices.reshape(8, 2, 4, 4, 2), CTX + MP)
    placed = (P(CTX, MP), P(CTX, MP), P(CTX, MP), P(MP, None), P(CTX, MP))
    return jax.shard_map(
        shards,
        mesh=fine,
        in_specs=placed,
        out_specs=(P(CTX, MP), P(CTX, MP), P(CTX, MP), P(CTX, MP), P(MP, None)),
        check_vma=False,
    )
```

```python
import functools

import jax
import jax.numpy as jnp
from jax import lax
from jax.experimental import pallas as pl
from jax.experimental.pallas import tpu as pltpu
from jax.sharding import Mesh, PartitionSpec as P

D = 8192
G = 16
K = 128
B = 16
FB = 32
W = 2 * K
LANES = 128
UNROLL = 4
LIMIT = 8 << 20
LOCAL_LIMIT = 107 << 19
TILE_GROUPS = LANES // G
CTX = ("y", "zl", "x")
MP = ("zh", "core")
HBM = pl.BlockSpec(memory_space=pl.ANY)
VMEM = pl.BlockSpec(memory_space=pltpu.VMEM)


def product_of(first, second):
    return (first.astype(jnp.float32) * second.astype(jnp.float32)).astype(jnp.bfloat16)


def blocks_of(rows, size):
    return jnp.concatenate([rows[n : n + size] for n in range(0, rows.shape[0], size)], axis=1)


def windows(rows, size):
    return jnp.concatenate([rows[n : n + W] for n in range(0, rows.shape[0] - W + size, size)], axis=1)


def group_of_lane(shape):
    return (lax.broadcasted_iota(jnp.int32, shape, 1) % LANES) // G


def correlate(product, following, tile, rows_ref):
    left = blocks_of(product, FB)
    group = group_of_lane(left.shape)
    zero = jnp.zeros_like(left)
    left = jnp.concatenate([jnp.where(group == g, left, zero) for g in range(TILE_GROUPS)], axis=0)
    pad = jnp.zeros((product.shape[0] - FB + W - following.shape[0], LANES), jnp.bfloat16)
    wins = windows(jnp.concatenate([following, pad], axis=0), FB)
    pairs = lax.dot_general(left, wins, (((1,), (1,)), ((), ())), preferred_element_type=jnp.float32)
    for g in range(TILE_GROUPS):
        total = pairs[g * FB : g * FB + 8]
        for r in range(8, FB, 8):
            total = total + pltpu.roll(pairs[g * FB + r : g * FB + r + 8], W - r, 1)
        rows_ref[pl.ds((tile * TILE_GROUPS + g) * 8, 8), :] = total


def fold(rows_ref):
    rows = rows_ref[...]
    sub = lax.broadcasted_iota(jnp.int32, rows.shape, 0)
    for bit in (1, 2, 4):
        rows = jnp.where((sub & bit) != 0, pltpu.roll(rows, W - bit, 1), rows)
    return jnp.sum(rows[:, :K].reshape(rows.shape[0] // 8, 8, K), axis=1)


def lanes_of(tile):
    return pl.ds(pl.multiple_of(tile * LANES, LANES), LANES)


def local_kernel(q_hbm, k_hbm, v_hbm, go_hbm, raw_ref, tail_ref, q_buf, k_buf, v_buf, go_buf, rows, sems):
    tokens, channels = q_buf.shape
    chunk = UNROLL * LANES

    def copies_of(i):
        c = pl.ds(pl.multiple_of(i * chunk, chunk), chunk)
        pairs = ((k_hbm, k_buf), (v_hbm, v_buf), (go_hbm, go_buf), (q_hbm, q_buf))
        return [pltpu.make_async_copy(src.at[:, c], dst.at[:, c], sems.at[n, i]) for n, (src, dst) in enumerate(pairs)]

    @pl.loop(0, channels // chunk)
    def _(i):
        for copy in copies_of(i):
            copy.start()

    @pl.loop(0, channels // chunk)
    def _(i):
        for copy in copies_of(i):
            copy.wait()
        for u in range(UNROLL):
            t = i * UNROLL + u
            c = lanes_of(t)
            product = product_of(k_buf[:, c], v_buf[:, c])
            tail_ref[:, c] = product[tokens - K :]
            correlate(product, product_of(go_buf[:, c], q_buf[:, c]), t, rows)

    raw_ref[...] = fold(rows)


def edge_kernel(tail_ref, after_ref, local_ref, raw_ref, rows):
    @pl.loop(0, tail_ref.shape[1] // LANES, unroll=UNROLL)
    def _(t):
        c = lanes_of(t)
        following = jnp.concatenate([jnp.zeros((K, LANES), jnp.bfloat16), after_ref[:, c]], axis=0)
        correlate(tail_ref[:, c], following, t, rows)

    raw_ref[...] = local_ref[...] + fold(rows)


def scale_kernel(raw_ref, squares_ref, out_ref):
    raw = raw_ref[...]
    mean = jnp.sum(squares_ref[...], axis=(0, 1), keepdims=True)[0]
    mean = jnp.sum(mean, axis=1, keepdims=True) / (D // G * K)
    out_ref[...] = raw * jnp.minimum(1.0, 1.0 / jnp.sqrt(mean + 1e-06))


def toeplitz_rows(rows_ref, t):
    mats = []
    for g in range(TILE_GROUPS):
        row = jnp.broadcast_to(rows_ref[pl.ds(t * TILE_GROUPS + g, 1), :], (B, W))
        mats.append(pltpu.roll(row, 0, 1, stride=1, stride_axis=0).astype(jnp.bfloat16))
    return jnp.concatenate(mats, axis=0)


def convolve(mats, rows):
    blocks = (rows.shape[0] - K) // B
    pad = jnp.zeros((W - K - B, LANES), jnp.bfloat16)
    wins = windows(jnp.concatenate([rows, pad], axis=0), B)
    full = jnp.dot(mats, wins, preferred_element_type=jnp.float32)
    group = group_of_lane((B, blocks * LANES))
    total = full[:B]
    for g in range(1, TILE_GROUPS):
        total = jnp.where(group == g, full[g * B : (g + 1) * B], total)
    total = total.astype(jnp.bfloat16).astype(jnp.float32)
    return jnp.concatenate([total[:, n * LANES : (n + 1) * LANES] for n in range(blocks)], axis=0)


def conv_kernel(causal, a_ref, b_ref, x_ref, y_ref, halo_ref, filter_ref, ox_hbm, oy_hbm, ox_buf, oy_buf, sems):
    tiles = a_ref.shape[1] // LANES

    def copies_of(t):
        c = lanes_of(t)
        pairs = ((ox_buf, ox_hbm), (oy_buf, oy_hbm))
        return [pltpu.make_async_copy(src.at[:, c], dst.at[:, c], sems.at[n, t]) for n, (src, dst) in enumerate(pairs)]

    @pl.loop(0, tiles, unroll=2)
    def _(t):
        c = lanes_of(t)
        own, halo = product_of(a_ref[:, c], b_ref[:, c]), halo_ref[:, c]
        out = convolve(toeplitz_rows(filter_ref, t), jnp.concatenate([halo, own] if causal else [own, halo], axis=0))
        ox_buf[:, c] = (out * x_ref[:, c].astype(jnp.float32)).astype(jnp.bfloat16)
        oy_buf[:, c] = (out * y_ref[:, c].astype(jnp.float32)).astype(jnp.bfloat16)
        for copy in copies_of(t):
            copy.start()

    @pl.loop(0, tiles)
    def _(t):
        for copy in copies_of(t):
            copy.wait()


def local_filter(q, k, v, go, slab_groups):
    return pl.pallas_call(
        local_kernel,
        in_specs=[HBM] * 4,
        out_specs=[VMEM] * 2,
        out_shape=[
            jax.ShapeDtypeStruct((slab_groups, K), jnp.float32),
            jax.ShapeDtypeStruct((K, q.shape[1]), jnp.bfloat16),
        ],
        scratch_shapes=[pltpu.VMEM(q.shape, jnp.bfloat16)] * 4
        + [
            pltpu.VMEM((slab_groups * 8, W), jnp.float32),
            pltpu.SemaphoreType.DMA((4, q.shape[1] // (UNROLL * LANES))),
        ],
        cost_estimate=pl.CostEstimate(flops=3 * 10**9, bytes_accessed=2**21, transcendentals=0),
        compiler_params=pltpu.CompilerParams(vmem_limit_bytes=LOCAL_LIMIT),
        name="local_filter",
    )(q, k, v, go)


def edge_filter(tail, after, local):
    return pl.pallas_call(
        edge_kernel,
        in_specs=[VMEM] * 3,
        out_specs=VMEM,
        out_shape=jax.ShapeDtypeStruct(local.shape, jnp.float32),
        scratch_shapes=[pltpu.VMEM((local.shape[0] * 8, W), jnp.float32)],
        cost_estimate=pl.CostEstimate(flops=10**9, bytes_accessed=2**19, transcendentals=0),
        compiler_params=pltpu.CompilerParams(vmem_limit_bytes=LIMIT),
        name="edge_filter",
    )(tail, after, local)


def conv(causal, signal, factors, halo, filter_rows):
    wide = jax.ShapeDtypeStruct(signal[0].shape, jnp.bfloat16)
    return pl.pallas_call(
        functools.partial(conv_kernel, causal),
        in_specs=[VMEM] * 6,
        out_specs=[HBM] * 2,
        out_shape=[wide] * 2,
        scratch_shapes=[pltpu.VMEM(wide.shape, jnp.bfloat16)] * 2
        + [pltpu.SemaphoreType.DMA((2, wide.shape[1] // LANES))],
        cost_estimate=pl.CostEstimate(flops=10**10, bytes_accessed=3 * 2**20, transcendentals=0),
        compiler_params=pltpu.CompilerParams(vmem_limit_bytes=LIMIT),
        name="forward_conv" if causal else "backward_conv",
    )(*signal, *factors, halo, filter_rows)


def scale(raw, squares):
    return pl.pallas_call(
        scale_kernel,
        in_specs=[VMEM] * 2,
        out_specs=VMEM,
        out_shape=jax.ShapeDtypeStruct(raw.shape, jnp.float32),
        compiler_params=pltpu.CompilerParams(vmem_limit_bytes=LIMIT),
        name="scale",
    )(raw, squares)


def spread_over(value, axes):
    size = lax.axis_size(axes)
    spread = jnp.broadcast_to(value[None], (size,) + value.shape)
    return lax.all_to_all(spread, axes, split_axis=0, concat_axis=0, tiled=True)


def shards(queries, key_feats, value_feats, filters, grad_out):
    slab_groups = filters.shape[0]
    owners = lax.axis_size(CTX)
    head = product_of(grad_out[:K], queries[:K])
    after = lax.ppermute(head, CTX, [(i + 1, i) for i in range(owners - 1)])
    local, tail = local_filter(queries, key_feats, value_feats, grad_out, slab_groups)
    raw = edge_filter(tail, after, local)

    filt = filters.astype(jnp.float32)
    zeros = jnp.zeros((slab_groups, W - K), jnp.float32)
    backward_rows = jnp.concatenate([filt, zeros], axis=1)
    forward_rows = jnp.concatenate([zeros[:, :1], filt[:, ::-1], zeros[:, 1:]], axis=1)

    before = lax.ppermute(tail, CTX, [(i, i + 1) for i in range(owners - 1)])
    before, after, _ = lax.optimization_barrier((before, after, raw))
    backward = conv(False, (grad_out, queries), (value_feats, key_feats), after, backward_rows)
    raw = jnp.sum(spread_over(raw, ("zl", "x")), axis=0)
    raw, backward = lax.optimization_barrier((raw, backward))
    before, _ = lax.optimization_barrier((before, raw))
    forward = conv(True, (key_feats, value_feats), (queries, grad_out), before, forward_rows)
    raw = jnp.sum(spread_over(raw, ("y",)), axis=0)
    raw, forward = lax.optimization_barrier((raw, forward))
    grad_filters = scale(raw, spread_over(jnp.sum(raw * raw, axis=0, keepdims=True), MP))
    return (*forward, *backward, grad_filters)


def solution(mesh):
    fine = Mesh(mesh.devices.reshape(8, 2, 4, 4, 2), CTX + MP)
    placed = (P(CTX, MP), P(CTX, MP), P(CTX, MP), P(MP, None), P(CTX, MP))
    return jax.shard_map(
        shards,
        mesh=fine,
        in_specs=placed,
        out_specs=(P(CTX, MP), P(CTX, MP), P(CTX, MP), P(CTX, MP), P(MP, None)),
        check_vma=False,
    )
```

```python
import functools

import jax
import jax.numpy as jnp
from jax import lax
from jax.experimental import pallas as pl
from jax.experimental.pallas import tpu as pltpu
from jax.sharding import Mesh, PartitionSpec as P

D = 8192
G = 16
K = 128
B = 16
FB = 32
W = 2 * K
LANES = 128
UNROLL = 4
LIMIT = 8 << 20
LOCAL_LIMIT = 107 << 19
TILE_GROUPS = LANES // G
CTX = ("y", "zl", "x")
MP = ("zh", "core")
HBM = pl.BlockSpec(memory_space=pl.ANY)
VMEM = pl.BlockSpec(memory_space=pltpu.VMEM)


def product_of(first, second):
    return (first.astype(jnp.float32) * second.astype(jnp.float32)).astype(jnp.bfloat16)


def blocks_of(rows, size):
    return jnp.concatenate([rows[n : n + size] for n in range(0, rows.shape[0], size)], axis=1)


def windows(rows, size):
    return jnp.concatenate([rows[n : n + W] for n in range(0, rows.shape[0] - W + size, size)], axis=1)


def group_of_lane(shape):
    return (lax.broadcasted_iota(jnp.int32, shape, 1) % LANES) // G


def correlate(product, following, tile, rows_ref):
    left = blocks_of(product, FB)
    group = group_of_lane(left.shape)
    zero = jnp.zeros_like(left)
    left = jnp.concatenate([jnp.where(group == g, left, zero) for g in range(TILE_GROUPS)], axis=0)
    pad = jnp.zeros((product.shape[0] - FB + W - following.shape[0], LANES), jnp.bfloat16)
    wins = windows(jnp.concatenate([following, pad], axis=0), FB)
    pairs = lax.dot_general(left, wins, (((1,), (1,)), ((), ())), preferred_element_type=jnp.float32)
    for g in range(TILE_GROUPS):
        total = pairs[g * FB : g * FB + 8]
        for r in range(8, FB, 8):
            total = total + pltpu.roll(pairs[g * FB + r : g * FB + r + 8], W - r, 1)
        rows_ref[pl.ds((tile * TILE_GROUPS + g) * 8, 8), :] = total


def fold(rows_ref):
    rows = rows_ref[...]
    sub = lax.broadcasted_iota(jnp.int32, rows.shape, 0)
    for bit in (1, 2, 4):
        rows = jnp.where((sub & bit) != 0, pltpu.roll(rows, W - bit, 1), rows)
    return jnp.sum(rows[:, :K].reshape(rows.shape[0] // 8, 8, K), axis=1)


def lanes_of(tile):
    return pl.ds(pl.multiple_of(tile * LANES, LANES), LANES)


def local_kernel(q_hbm, k_hbm, v_hbm, go_hbm, raw_ref, tail_ref, q_buf, k_buf, v_buf, go_buf, rows, sems):
    tokens, channels = q_buf.shape
    chunk = UNROLL * LANES

    def copies_of(i):
        c = pl.ds(pl.multiple_of(i * chunk, chunk), chunk)
        pairs = ((k_hbm, k_buf), (v_hbm, v_buf), (go_hbm, go_buf), (q_hbm, q_buf))
        return [pltpu.make_async_copy(src.at[:, c], dst.at[:, c], sems.at[n, i]) for n, (src, dst) in enumerate(pairs)]

    @pl.loop(0, channels // chunk)
    def _(i):
        for copy in copies_of(i):
            copy.start()

    @pl.loop(0, channels // chunk)
    def _(i):
        for copy in copies_of(i):
            copy.wait()
        for u in range(UNROLL):
            t = i * UNROLL + u
            c = lanes_of(t)
            product = product_of(k_buf[:, c], v_buf[:, c])
            tail_ref[:, c] = product[tokens - K :]
            correlate(product, product_of(go_buf[:, c], q_buf[:, c]), t, rows)

    raw_ref[...] = fold(rows)


def edge_kernel(tail_ref, after_ref, local_ref, raw_ref, rows):
    @pl.loop(0, tail_ref.shape[1] // LANES, unroll=UNROLL)
    def _(t):
        c = lanes_of(t)
        following = jnp.concatenate([jnp.zeros((K, LANES), jnp.bfloat16), after_ref[:, c]], axis=0)
        correlate(tail_ref[:, c], following, t, rows)

    raw_ref[...] = local_ref[...] + fold(rows)


def scale_kernel(raw_ref, squares_ref, out_ref):
    raw = raw_ref[...]
    mean = jnp.sum(squares_ref[...], axis=(0, 1), keepdims=True)[0]
    mean = jnp.sum(mean, axis=1, keepdims=True) / (D // G * K)
    out_ref[...] = raw * jnp.minimum(1.0, 1.0 / jnp.sqrt(mean + 1e-06))


def toeplitz_rows(rows_ref, t):
    mats = []
    for g in range(TILE_GROUPS):
        row = jnp.broadcast_to(rows_ref[pl.ds(t * TILE_GROUPS + g, 1), :], (B, W))
        mats.append(pltpu.roll(row, 0, 1, stride=1, stride_axis=0).astype(jnp.bfloat16))
    return jnp.concatenate(mats, axis=0)


def convolve(mats, rows):
    blocks = (rows.shape[0] - K) // B
    pad = jnp.zeros((W - K - B, LANES), jnp.bfloat16)
    wins = windows(jnp.concatenate([rows, pad], axis=0), B)
    full = jnp.dot(mats, wins, preferred_element_type=jnp.float32)
    group = group_of_lane((B, blocks * LANES))
    total = full[:B]
    for g in range(1, TILE_GROUPS):
        total = jnp.where(group == g, full[g * B : (g + 1) * B], total)
    total = total.astype(jnp.bfloat16).astype(jnp.float32)
    return jnp.concatenate([total[:, n * LANES : (n + 1) * LANES] for n in range(blocks)], axis=0)


def conv_kernel(causal, a_ref, b_ref, x_ref, y_ref, halo_ref, filter_ref, ox_hbm, oy_hbm, ox_buf, oy_buf, sems):
    tiles = a_ref.shape[1] // LANES

    def copies_of(t):
        c = lanes_of(t)
        pairs = ((ox_buf, ox_hbm), (oy_buf, oy_hbm))
        return [pltpu.make_async_copy(src.at[:, c], dst.at[:, c], sems.at[n, t]) for n, (src, dst) in enumerate(pairs)]

    @pl.loop(0, tiles, unroll=2)
    def _(t):
        c = lanes_of(t)
        own, halo = product_of(a_ref[:, c], b_ref[:, c]), halo_ref[:, c]
        out = convolve(toeplitz_rows(filter_ref, t), jnp.concatenate([halo, own] if causal else [own, halo], axis=0))
        ox_buf[:, c] = (out * x_ref[:, c].astype(jnp.float32)).astype(jnp.bfloat16)
        oy_buf[:, c] = (out * y_ref[:, c].astype(jnp.float32)).astype(jnp.bfloat16)
        for copy in copies_of(t):
            copy.start()

    @pl.loop(0, tiles)
    def _(t):
        for copy in copies_of(t):
            copy.wait()


def local_filter(q, k, v, go, slab_groups):
    return pl.pallas_call(
        local_kernel,
        in_specs=[HBM] * 4,
        out_specs=[VMEM] * 2,
        out_shape=[
            jax.ShapeDtypeStruct((slab_groups, K), jnp.float32),
            jax.ShapeDtypeStruct((K, q.shape[1]), jnp.bfloat16),
        ],
        scratch_shapes=[pltpu.VMEM(q.shape, jnp.bfloat16)] * 4
        + [
            pltpu.VMEM((slab_groups * 8, W), jnp.float32),
            pltpu.SemaphoreType.DMA((4, q.shape[1] // (UNROLL * LANES))),
        ],
        cost_estimate=pl.CostEstimate(flops=3 * 10**9, bytes_accessed=2**21, transcendentals=0),
        compiler_params=pltpu.CompilerParams(vmem_limit_bytes=LOCAL_LIMIT),
        name="local_filter",
    )(q, k, v, go)


def edge_filter(tail, after, local):
    return pl.pallas_call(
        edge_kernel,
        in_specs=[VMEM] * 3,
        out_specs=VMEM,
        out_shape=jax.ShapeDtypeStruct(local.shape, jnp.float32),
        scratch_shapes=[pltpu.VMEM((local.shape[0] * 8, W), jnp.float32)],
        cost_estimate=pl.CostEstimate(flops=10**9, bytes_accessed=2**19, transcendentals=0),
        compiler_params=pltpu.CompilerParams(vmem_limit_bytes=LIMIT),
        name="edge_filter",
    )(tail, after, local)


def conv(causal, signal, factors, halo, filter_rows):
    wide = jax.ShapeDtypeStruct(signal[0].shape, jnp.bfloat16)
    return pl.pallas_call(
        functools.partial(conv_kernel, causal),
        in_specs=[VMEM] * 6,
        out_specs=[HBM] * 2,
        out_shape=[wide] * 2,
        scratch_shapes=[pltpu.VMEM(wide.shape, jnp.bfloat16)] * 2
        + [pltpu.SemaphoreType.DMA((2, wide.shape[1] // LANES))],
        cost_estimate=pl.CostEstimate(flops=10**10, bytes_accessed=3 * 2**20, transcendentals=0),
        compiler_params=pltpu.CompilerParams(vmem_limit_bytes=LIMIT),
        name="forward_conv" if causal else "backward_conv",
    )(*signal, *factors, halo, filter_rows)


def scale(raw, squares):
    return pl.pallas_call(
        scale_kernel,
        in_specs=[VMEM] * 2,
        out_specs=VMEM,
        out_shape=jax.ShapeDtypeStruct(raw.shape, jnp.float32),
        compiler_params=pltpu.CompilerParams(vmem_limit_bytes=LIMIT),
        name="scale",
    )(raw, squares)


def spread_over(value, axes, groups=None):
    size = len(groups[0]) if groups else lax.axis_size(axes)
    spread = jnp.broadcast_to(value[None], (size,) + value.shape)
    return lax.all_to_all(spread, axes, split_axis=0, concat_axis=0, tiled=True, axis_index_groups=groups)


def slab_groups_along_z():
    highs, cores = lax.axis_size("zh"), lax.axis_size("core")

    def index(z, core):
        return ((z % 2) * highs + z // 2) * cores + core

    return [[index(z, core) for z in chips for core in range(cores)] for chips in ((1, 2, 4, 7), (0, 3, 5, 6))]


def shards(queries, key_feats, value_feats, filters, grad_out):
    slab_groups = filters.shape[0]
    owners = lax.axis_size(CTX)
    head = product_of(grad_out[:K], queries[:K])
    after = lax.ppermute(head, CTX, [(i + 1, i) for i in range(owners - 1)])
    local, tail = local_filter(queries, key_feats, value_feats, grad_out, slab_groups)
    raw = edge_filter(tail, after, local)

    filt = filters.astype(jnp.float32)
    zeros = jnp.zeros((slab_groups, W - K), jnp.float32)
    backward_rows = jnp.concatenate([filt, zeros], axis=1)
    forward_rows = jnp.concatenate([zeros[:, :1], filt[:, ::-1], zeros[:, 1:]], axis=1)

    before = lax.ppermute(tail, CTX, [(i, i + 1) for i in range(owners - 1)])
    before, after, _ = lax.optimization_barrier((before, after, raw))
    backward = conv(False, (grad_out, queries), (value_feats, key_feats), after, backward_rows)
    raw = jnp.sum(spread_over(raw, ("zl", "x")), axis=0)
    raw, backward = lax.optimization_barrier((raw, backward))
    before, _ = lax.optimization_barrier((before, raw))
    forward = conv(True, (key_feats, value_feats), (queries, grad_out), before, forward_rows)
    raw = jnp.sum(spread_over(raw, ("y",)), axis=0)
    raw, forward = lax.optimization_barrier((raw, forward))
    grad_filters = scale(raw, spread_over(jnp.sum(raw * raw, axis=0, keepdims=True), ("zl",) + MP, slab_groups_along_z()))
    return (*forward, *backward, grad_filters)


def solution(mesh):
    fine = Mesh(mesh.devices.reshape(8, 2, 4, 4, 2), CTX + MP)
    placed = (P(CTX, MP), P(CTX, MP), P(CTX, MP), P(MP, None), P(CTX, MP))
    return jax.shard_map(
        shards,
        mesh=fine,
        in_specs=placed,
        out_specs=(P(CTX, MP), P(CTX, MP), P(CTX, MP), P(CTX, MP), P(MP, None)),
        check_vma=False,
    )
```

```python
import functools

import jax
import jax.numpy as jnp
from jax import lax
from jax.experimental import pallas as pl
from jax.experimental.pallas import tpu as pltpu
from jax.sharding import Mesh, PartitionSpec as P

D = 8192
G = 16
K = 128
B = 16
FB = 32
W = 2 * K
LANES = 128
UNROLL = 4
LIMIT = 8 << 20
LOCAL_LIMIT = 107 << 19
TILE_GROUPS = LANES // G
CTX = ("y", "zl", "x")
MP = ("zh", "core")
HBM = pl.BlockSpec(memory_space=pl.ANY)
VMEM = pl.BlockSpec(memory_space=pltpu.VMEM)


def product_of(first, second):
    return (first.astype(jnp.float32) * second.astype(jnp.float32)).astype(jnp.bfloat16)


def blocks_of(rows, size):
    return jnp.concatenate([rows[n : n + size] for n in range(0, rows.shape[0], size)], axis=1)


def windows(rows, size):
    return jnp.concatenate([rows[n : n + W] for n in range(0, rows.shape[0] - W + size, size)], axis=1)


def group_of_lane(shape):
    return (lax.broadcasted_iota(jnp.int32, shape, 1) % LANES) // G


def correlate(product, following, tile, rows_ref):
    left = blocks_of(product, FB)
    group = group_of_lane(left.shape)
    zero = jnp.zeros_like(left)
    left = jnp.concatenate([jnp.where(group == g, left, zero) for g in range(TILE_GROUPS)], axis=0)
    pad = jnp.zeros((product.shape[0] - FB + W - following.shape[0], LANES), jnp.bfloat16)
    wins = windows(jnp.concatenate([following, pad], axis=0), FB)
    pairs = lax.dot_general(left, wins, (((1,), (1,)), ((), ())), preferred_element_type=jnp.float32)
    for g in range(TILE_GROUPS):
        total = pairs[g * FB : g * FB + 8]
        for r in range(8, FB, 8):
            total = total + pltpu.roll(pairs[g * FB + r : g * FB + r + 8], W - r, 1)
        rows_ref[pl.ds((tile * TILE_GROUPS + g) * 8, 8), :] = total


def fold(rows_ref):
    rows = rows_ref[...]
    sub = lax.broadcasted_iota(jnp.int32, rows.shape, 0)
    for bit in (1, 2, 4):
        rows = jnp.where((sub & bit) != 0, pltpu.roll(rows, W - bit, 1), rows)
    return jnp.sum(rows[:, :K].reshape(rows.shape[0] // 8, 8, K), axis=1)


def lanes_of(tile):
    return pl.ds(pl.multiple_of(tile * LANES, LANES), LANES)


def local_kernel(q_hbm, k_hbm, v_hbm, go_hbm, raw_ref, tail_ref, q_buf, k_buf, v_buf, go_buf, rows, sems):
    tokens, channels = q_buf.shape
    chunk = UNROLL * LANES

    def copies_of(i):
        c = pl.ds(pl.multiple_of(i * chunk, chunk), chunk)
        pairs = ((k_hbm, k_buf), (v_hbm, v_buf), (go_hbm, go_buf), (q_hbm, q_buf))
        return [pltpu.make_async_copy(src.at[:, c], dst.at[:, c], sems.at[n, i]) for n, (src, dst) in enumerate(pairs)]

    @pl.loop(0, channels // chunk)
    def _(i):
        for copy in copies_of(i):
            copy.start()

    @pl.loop(0, channels // chunk)
    def _(i):
        for copy in copies_of(i):
            copy.wait()
        for u in range(UNROLL):
            t = i * UNROLL + u
            c = lanes_of(t)
            product = product_of(k_buf[:, c], v_buf[:, c])
            tail_ref[:, c] = product[tokens - K :]
            correlate(product, product_of(go_buf[:, c], q_buf[:, c]), t, rows)

    raw_ref[...] = fold(rows)


def edge_kernel(tail_ref, after_ref, local_ref, raw_ref, rows):
    for t in range(tail_ref.shape[1] // LANES):
        c = slice(t * LANES, (t + 1) * LANES)
        following = jnp.concatenate([jnp.zeros((K, LANES), jnp.bfloat16), after_ref[:, c]], axis=0)
        correlate(tail_ref[:, c], following, t, rows)

    raw_ref[...] = local_ref[...] + fold(rows)


def scale_kernel(raw_ref, squares_ref, out_ref):
    raw = raw_ref[...]
    mean = jnp.sum(squares_ref[...], axis=(0, 1), keepdims=True)[0]
    mean = jnp.sum(mean, axis=1, keepdims=True) / (D // G * K)
    out_ref[...] = raw * jnp.minimum(1.0, 1.0 / jnp.sqrt(mean + 1e-06))


def toeplitz_rows(rows_ref, t):
    mats = []
    for g in range(TILE_GROUPS):
        row = jnp.broadcast_to(rows_ref[pl.ds(t * TILE_GROUPS + g, 1), :], (B, W))
        mats.append(pltpu.roll(row, 0, 1, stride=1, stride_axis=0).astype(jnp.bfloat16))
    return jnp.concatenate(mats, axis=0)


def convolve(mats, rows):
    blocks = (rows.shape[0] - K) // B
    pad = jnp.zeros((W - K - B, LANES), jnp.bfloat16)
    wins = windows(jnp.concatenate([rows, pad], axis=0), B)
    full = jnp.dot(mats, wins, preferred_element_type=jnp.float32)
    group = group_of_lane((B, blocks * LANES))
    total = full[:B]
    for g in range(1, TILE_GROUPS):
        total = jnp.where(group == g, full[g * B : (g + 1) * B], total)
    total = total.astype(jnp.bfloat16).astype(jnp.float32)
    return jnp.concatenate([total[:, n * LANES : (n + 1) * LANES] for n in range(blocks)], axis=0)


def conv_kernel(causal, a_ref, b_ref, x_ref, y_ref, halo_ref, filter_ref, ox_hbm, oy_hbm, ox_buf, oy_buf, sems):
    tiles = a_ref.shape[1] // LANES

    def copies_of(t):
        c = lanes_of(t)
        pairs = ((ox_buf, ox_hbm), (oy_buf, oy_hbm))
        return [pltpu.make_async_copy(src.at[:, c], dst.at[:, c], sems.at[n, t]) for n, (src, dst) in enumerate(pairs)]

    @pl.loop(0, tiles, unroll=2)
    def _(t):
        c = lanes_of(t)
        own, halo = product_of(a_ref[:, c], b_ref[:, c]), halo_ref[:, c]
        out = convolve(toeplitz_rows(filter_ref, t), jnp.concatenate([halo, own] if causal else [own, halo], axis=0))
        ox_buf[:, c] = (out * x_ref[:, c].astype(jnp.float32)).astype(jnp.bfloat16)
        oy_buf[:, c] = (out * y_ref[:, c].astype(jnp.float32)).astype(jnp.bfloat16)
        for copy in copies_of(t):
            copy.start()

    @pl.loop(0, tiles)
    def _(t):
        for copy in copies_of(t):
            copy.wait()


def local_filter(q, k, v, go, slab_groups):
    return pl.pallas_call(
        local_kernel,
        in_specs=[HBM] * 4,
        out_specs=[VMEM] * 2,
        out_shape=[
            jax.ShapeDtypeStruct((slab_groups, K), jnp.float32),
            jax.ShapeDtypeStruct((K, q.shape[1]), jnp.bfloat16),
        ],
        scratch_shapes=[pltpu.VMEM(q.shape, jnp.bfloat16)] * 4
        + [
            pltpu.VMEM((slab_groups * 8, W), jnp.float32),
            pltpu.SemaphoreType.DMA((4, q.shape[1] // (UNROLL * LANES))),
        ],
        cost_estimate=pl.CostEstimate(flops=3 * 10**9, bytes_accessed=2**21, transcendentals=0),
        compiler_params=pltpu.CompilerParams(vmem_limit_bytes=LOCAL_LIMIT),
        name="local_filter",
    )(q, k, v, go)


def edge_filter(tail, after, local):
    return pl.pallas_call(
        edge_kernel,
        in_specs=[VMEM] * 3,
        out_specs=VMEM,
        out_shape=jax.ShapeDtypeStruct(local.shape, jnp.float32),
        scratch_shapes=[pltpu.VMEM((local.shape[0] * 8, W), jnp.float32)],
        cost_estimate=pl.CostEstimate(flops=10**9, bytes_accessed=2**19, transcendentals=0),
        compiler_params=pltpu.CompilerParams(vmem_limit_bytes=LIMIT),
        name="edge_filter",
    )(tail, after, local)


def conv(causal, signal, factors, halo, filter_rows):
    wide = jax.ShapeDtypeStruct(signal[0].shape, jnp.bfloat16)
    return pl.pallas_call(
        functools.partial(conv_kernel, causal),
        in_specs=[VMEM] * 6,
        out_specs=[HBM] * 2,
        out_shape=[wide] * 2,
        scratch_shapes=[pltpu.VMEM(wide.shape, jnp.bfloat16)] * 2
        + [pltpu.SemaphoreType.DMA((2, wide.shape[1] // LANES))],
        cost_estimate=pl.CostEstimate(flops=10**10, bytes_accessed=3 * 2**20, transcendentals=0),
        compiler_params=pltpu.CompilerParams(vmem_limit_bytes=LIMIT),
        name="forward_conv" if causal else "backward_conv",
    )(*signal, *factors, halo, filter_rows)


def scale(raw, squares):
    return pl.pallas_call(
        scale_kernel,
        in_specs=[VMEM] * 2,
        out_specs=VMEM,
        out_shape=jax.ShapeDtypeStruct(raw.shape, jnp.float32),
        compiler_params=pltpu.CompilerParams(vmem_limit_bytes=LIMIT),
        name="scale",
    )(raw, squares)


def spread_over(value, axes, groups=None):
    size = len(groups[0]) if groups else lax.axis_size(axes)
    spread = jnp.broadcast_to(value[None], (size,) + value.shape)
    return lax.all_to_all(spread, axes, split_axis=0, concat_axis=0, tiled=True, axis_index_groups=groups)


def slab_groups_along_z():
    highs, cores = lax.axis_size("zh"), lax.axis_size("core")

    def index(z, core):
        return ((z % 2) * highs + z // 2) * cores + core

    return [[index(z, core) for z in chips for core in range(cores)] for chips in ((1, 2, 4, 7), (0, 3, 5, 6))]


def shards(queries, key_feats, value_feats, filters, grad_out):
    slab_groups = filters.shape[0]
    owners = lax.axis_size(CTX)
    head = product_of(grad_out[:K], queries[:K])
    after = lax.ppermute(head, CTX, [(i + 1, i) for i in range(owners - 1)])
    local, tail = local_filter(queries, key_feats, value_feats, grad_out, slab_groups)
    raw = edge_filter(tail, after, local)

    filt = filters.astype(jnp.float32)
    zeros = jnp.zeros((slab_groups, W - K), jnp.float32)
    backward_rows = jnp.concatenate([filt, zeros], axis=1)
    forward_rows = jnp.concatenate([zeros[:, :1], filt[:, ::-1], zeros[:, 1:]], axis=1)

    before = lax.ppermute(tail, CTX, [(i, i + 1) for i in range(owners - 1)])
    before, after, _ = lax.optimization_barrier((before, after, raw))
    backward = conv(False, (grad_out, queries), (value_feats, key_feats), after, backward_rows)
    raw = jnp.sum(spread_over(raw, ("zl", "x")), axis=0)
    raw, backward = lax.optimization_barrier((raw, backward))
    before, _ = lax.optimization_barrier((before, raw))
    forward = conv(True, (key_feats, value_feats), (queries, grad_out), before, forward_rows)
    raw = jnp.sum(spread_over(raw, ("y",)), axis=0)
    raw, forward = lax.optimization_barrier((raw, forward))
    grad_filters = scale(raw, spread_over(jnp.sum(raw * raw, axis=0, keepdims=True), ("zl",) + MP, slab_groups_along_z()))
    return (*forward, *backward, grad_filters)


def solution(mesh):
    fine = Mesh(mesh.devices.reshape(8, 2, 4, 4, 2), CTX + MP)
    placed = (P(CTX, MP), P(CTX, MP), P(CTX, MP), P(MP, None), P(CTX, MP))
    return jax.shard_map(
        shards,
        mesh=fine,
        in_specs=placed,
        out_specs=(P(CTX, MP), P(CTX, MP), P(CTX, MP), P(CTX, MP), P(MP, None)),
        check_vma=False,
    )
```

```python
import functools

import jax
import jax.numpy as jnp
from jax import lax
from jax.experimental import pallas as pl
from jax.experimental.pallas import tpu as pltpu
from jax.sharding import Mesh, PartitionSpec as P

D = 8192
G = 16
K = 128
B = 16
FB = 32
W = 2 * K
LANES = 128
LIMIT = 8 << 20
CHUNK = 4
LOCAL_LIMIT = 107 << 19
TILE_GROUPS = LANES // G
CTX = ("y", "zl", "x")
MP = ("zh", "core")
HBM = pl.BlockSpec(memory_space=pl.ANY)
VMEM = pl.BlockSpec(memory_space=pltpu.VMEM)


def product_of(first, second):
    return (first.astype(jnp.float32) * second.astype(jnp.float32)).astype(jnp.bfloat16)


def blocks_of(rows, size):
    return jnp.concatenate([rows[n : n + size] for n in range(0, rows.shape[0], size)], axis=1)


def windows(rows, size):
    return jnp.concatenate([rows[n : n + W] for n in range(0, rows.shape[0] - W + size, size)], axis=1)


def group_of_lane(shape):
    return (lax.broadcasted_iota(jnp.int32, shape, 1) % LANES) // G


def correlate(product, following, tile, rows_ref):
    left = blocks_of(product, FB)
    group = group_of_lane(left.shape)
    zero = jnp.zeros_like(left)
    left = jnp.concatenate([jnp.where(group == g, left, zero) for g in range(TILE_GROUPS)], axis=0)
    pad = jnp.zeros((product.shape[0] - FB + W - following.shape[0], LANES), jnp.bfloat16)
    wins = windows(jnp.concatenate([following, pad], axis=0), FB)
    pairs = lax.dot_general(left, wins, (((1,), (1,)), ((), ())), preferred_element_type=jnp.float32)
    for g in range(TILE_GROUPS):
        total = pairs[g * FB : g * FB + 8]
        for r in range(8, FB, 8):
            total = total + pltpu.roll(pairs[g * FB + r : g * FB + r + 8], W - r, 1)
        rows_ref[pl.ds((tile * TILE_GROUPS + g) * 8, 8), :] = total


def fold(rows_ref):
    rows = rows_ref[...]
    sub = lax.broadcasted_iota(jnp.int32, rows.shape, 0)
    for bit in (1, 2, 4):
        rows = jnp.where((sub & bit) != 0, pltpu.roll(rows, W - bit, 1), rows)
    return jnp.sum(rows[:, :K].reshape(rows.shape[0] // 8, 8, K), axis=1)


def lanes_of(tile):
    return pl.ds(pl.multiple_of(tile * LANES, LANES), LANES)


def local_kernel(q_hbm, k_hbm, v_hbm, go_hbm, raw_ref, tail_ref, q_buf, k_buf, v_buf, go_buf, rows, sems):
    tokens, channels = q_buf.shape
    chunk = CHUNK * LANES
    pairs = ((k_hbm, k_buf), (v_hbm, v_buf), (go_hbm, go_buf), (q_hbm, q_buf))
    copies = [
        [
            pltpu.make_async_copy(src.at[:, i : i + chunk], dst.at[:, i : i + chunk], sems.at[n, i // chunk])
            for n, (src, dst) in enumerate(pairs)
        ]
        for i in range(0, channels, chunk)
    ]
    for group in copies:
        for copy in group:
            copy.start()
    for t in range(channels // LANES):
        if t % CHUNK == 0:
            for copy in copies[t // CHUNK]:
                copy.wait()
        c = slice(t * LANES, (t + 1) * LANES)
        product = product_of(k_buf[:, c], v_buf[:, c])
        tail_ref[:, c] = product[tokens - K :]
        correlate(product, product_of(go_buf[:, c], q_buf[:, c]), t, rows)

    raw_ref[...] = fold(rows)


def edge_kernel(tail_ref, after_ref, local_ref, raw_ref, rows):
    for t in range(tail_ref.shape[1] // LANES):
        c = slice(t * LANES, (t + 1) * LANES)
        following = jnp.concatenate([jnp.zeros((K, LANES), jnp.bfloat16), after_ref[:, c]], axis=0)
        correlate(tail_ref[:, c], following, t, rows)

    raw_ref[...] = local_ref[...] + fold(rows)


def scale_kernel(raw_ref, squares_ref, out_ref):
    raw = raw_ref[...]
    mean = jnp.sum(squares_ref[...], axis=(0, 1), keepdims=True)[0]
    mean = jnp.sum(mean, axis=1, keepdims=True) / (D // G * K)
    out_ref[...] = raw * jnp.minimum(1.0, 1.0 / jnp.sqrt(mean + 1e-06))


def toeplitz_rows(rows_ref, t):
    mats = []
    for g in range(TILE_GROUPS):
        row = jnp.broadcast_to(rows_ref[pl.ds(t * TILE_GROUPS + g, 1), :], (B, W))
        mats.append(pltpu.roll(row, 0, 1, stride=1, stride_axis=0).astype(jnp.bfloat16))
    return jnp.concatenate(mats, axis=0)


def convolve(mats, rows):
    blocks = (rows.shape[0] - K) // B
    pad = jnp.zeros((W - K - B, LANES), jnp.bfloat16)
    wins = windows(jnp.concatenate([rows, pad], axis=0), B)
    full = jnp.dot(mats, wins, preferred_element_type=jnp.float32)
    group = group_of_lane((B, blocks * LANES))
    total = full[:B]
    for g in range(1, TILE_GROUPS):
        total = jnp.where(group == g, full[g * B : (g + 1) * B], total)
    total = total.astype(jnp.bfloat16).astype(jnp.float32)
    return jnp.concatenate([total[:, n * LANES : (n + 1) * LANES] for n in range(blocks)], axis=0)


def conv_kernel(causal, a_ref, b_ref, x_ref, y_ref, halo_ref, filter_ref, ox_hbm, oy_hbm, ox_buf, oy_buf, sems):
    tiles = a_ref.shape[1] // LANES

    def copies_of(t):
        c = lanes_of(t)
        pairs = ((ox_buf, ox_hbm), (oy_buf, oy_hbm))
        return [pltpu.make_async_copy(src.at[:, c], dst.at[:, c], sems.at[n, t]) for n, (src, dst) in enumerate(pairs)]

    @pl.loop(0, tiles, unroll=2)
    def _(t):
        c = lanes_of(t)
        own, halo = product_of(a_ref[:, c], b_ref[:, c]), halo_ref[:, c]
        out = convolve(toeplitz_rows(filter_ref, t), jnp.concatenate([halo, own] if causal else [own, halo], axis=0))
        ox_buf[:, c] = (out * x_ref[:, c].astype(jnp.float32)).astype(jnp.bfloat16)
        oy_buf[:, c] = (out * y_ref[:, c].astype(jnp.float32)).astype(jnp.bfloat16)
        for copy in copies_of(t):
            copy.start()

    @pl.loop(0, tiles)
    def _(t):
        for copy in copies_of(t):
            copy.wait()


def local_filter(q, k, v, go, slab_groups):
    return pl.pallas_call(
        local_kernel,
        in_specs=[HBM] * 4,
        out_specs=[VMEM] * 2,
        out_shape=[
            jax.ShapeDtypeStruct((slab_groups, K), jnp.float32),
            jax.ShapeDtypeStruct((K, q.shape[1]), jnp.bfloat16),
        ],
        scratch_shapes=[pltpu.VMEM(q.shape, jnp.bfloat16)] * 4
        + [
            pltpu.VMEM((slab_groups * 8, W), jnp.float32),
            pltpu.SemaphoreType.DMA((4, q.shape[1] // (CHUNK * LANES))),
        ],
        cost_estimate=pl.CostEstimate(flops=3 * 10**9, bytes_accessed=2**21, transcendentals=0),
        compiler_params=pltpu.CompilerParams(vmem_limit_bytes=LOCAL_LIMIT),
        name="local_filter",
    )(q, k, v, go)


def edge_filter(tail, after, local):
    return pl.pallas_call(
        edge_kernel,
        in_specs=[VMEM] * 3,
        out_specs=VMEM,
        out_shape=jax.ShapeDtypeStruct(local.shape, jnp.float32),
        scratch_shapes=[pltpu.VMEM((local.shape[0] * 8, W), jnp.float32)],
        cost_estimate=pl.CostEstimate(flops=10**9, bytes_accessed=2**19, transcendentals=0),
        compiler_params=pltpu.CompilerParams(vmem_limit_bytes=LIMIT),
        name="edge_filter",
    )(tail, after, local)


def conv(causal, signal, factors, halo, filter_rows):
    wide = jax.ShapeDtypeStruct(signal[0].shape, jnp.bfloat16)
    return pl.pallas_call(
        functools.partial(conv_kernel, causal),
        in_specs=[VMEM] * 6,
        out_specs=[HBM] * 2,
        out_shape=[wide] * 2,
        scratch_shapes=[pltpu.VMEM(wide.shape, jnp.bfloat16)] * 2
        + [pltpu.SemaphoreType.DMA((2, wide.shape[1] // LANES))],
        cost_estimate=pl.CostEstimate(flops=10**10, bytes_accessed=3 * 2**20, transcendentals=0),
        compiler_params=pltpu.CompilerParams(vmem_limit_bytes=LIMIT),
        name="forward_conv" if causal else "backward_conv",
    )(*signal, *factors, halo, filter_rows)


def scale(raw, squares):
    return pl.pallas_call(
        scale_kernel,
        in_specs=[VMEM] * 2,
        out_specs=VMEM,
        out_shape=jax.ShapeDtypeStruct(raw.shape, jnp.float32),
        compiler_params=pltpu.CompilerParams(vmem_limit_bytes=LIMIT),
        name="scale",
    )(raw, squares)


def spread_over(value, axes, groups=None):
    size = len(groups[0]) if groups else lax.axis_size(axes)
    spread = jnp.broadcast_to(value[None], (size,) + value.shape)
    return lax.all_to_all(spread, axes, split_axis=0, concat_axis=0, tiled=True, axis_index_groups=groups)


def slab_groups_along_z():
    highs, cores = lax.axis_size("zh"), lax.axis_size("core")

    def index(z, core):
        return ((z % 2) * highs + z // 2) * cores + core

    return [[index(z, core) for z in chips for core in range(cores)] for chips in ((1, 2, 4, 7), (0, 3, 5, 6))]


def shards(queries, key_feats, value_feats, filters, grad_out):
    slab_groups = filters.shape[0]
    owners = lax.axis_size(CTX)
    head = product_of(grad_out[:K], queries[:K])
    after = lax.ppermute(head, CTX, [(i + 1, i) for i in range(owners - 1)])
    local, tail = local_filter(queries, key_feats, value_feats, grad_out, slab_groups)
    raw = edge_filter(tail, after, local)

    filters, _ = lax.optimization_barrier((filters, raw))
    filt = filters.astype(jnp.float32)
    zeros = jnp.zeros((slab_groups, W - K), jnp.float32)
    backward_rows = jnp.concatenate([filt, zeros], axis=1)
    forward_rows = jnp.concatenate([zeros[:, :1], filt[:, ::-1], zeros[:, 1:]], axis=1)

    before = lax.ppermute(tail, CTX, [(i, i + 1) for i in range(owners - 1)])
    before, after, _ = lax.optimization_barrier((before, after, raw))
    backward = conv(False, (grad_out, queries), (value_feats, key_feats), after, backward_rows)
    raw = jnp.sum(spread_over(raw, ("zl", "x")), axis=0)
    raw, backward = lax.optimization_barrier((raw, backward))
    before, _ = lax.optimization_barrier((before, raw))
    forward = conv(True, (key_feats, value_feats), (queries, grad_out), before, forward_rows)
    raw = jnp.sum(spread_over(raw, ("y",)), axis=0)
    raw, forward = lax.optimization_barrier((raw, forward))
    grad_filters = scale(raw, spread_over(jnp.sum(raw * raw, axis=0, keepdims=True), ("zl",) + MP, slab_groups_along_z()))
    return (*forward, *backward, grad_filters)


def solution(mesh):
    fine = Mesh(mesh.devices.reshape(8, 2, 4, 4, 2), CTX + MP)
    placed = (P(CTX, MP), P(CTX, MP), P(CTX, MP), P(MP, None), P(CTX, MP))
    return jax.shard_map(
        shards,
        mesh=fine,
        in_specs=placed,
        out_specs=(P(CTX, MP), P(CTX, MP), P(CTX, MP), P(CTX, MP), P(MP, None)),
        check_vma=False,
    )
```
